256 devices in a mesh: ex: 16 (over y_hi, z), feat: 16 (over x, y_lo, core).
Axes of the slice: x: 4, y: 4 (y_hi: 2, y_lo: 2; y = y_hi * 2 + y_lo), z: 8, core: 2. Of those that a mesh axis runs over, the one named last changes fastest.
Arguments:
- grads: float32 [16384, 32768], P('ex', 'feat'), may hold values from -0.44595265 to 0.44595265
- resid: float32 [16384], P('ex'), may hold values from 0.1 to 1
- offsets: int32 [3], replicated, may hold values from 0 to 512
Outputs:
- kernel: float32 [3, 512, 16384], P(None, 'feat', 'ex')
The draws below stay inside these ranges and needn't reach their ends.
All inputs are finite; a program needn't handle non-finite values.
Results may differ from the reference program's by a relative error of at most 0.00015.
Values sent between devices are 32-bit elements; how exact they have to be, the bound alone decides.
A program may use at most 64 MiB of HBM per device.

```python
import math
import jax
import jax.numpy as jnp
from jax import lax

P_SIZE = 32768
RES_DEV = 1024
GROUP = 512
STEPS = 3
EXAMPLES = 16384
N_EX = 16


def levels(own_key, dims, split, smallest, largest):
    def one(dim, parts):
        heights = jax.random.uniform(jax.random.fold_in(jax.random.fold_in(own_key, 6), dim), (parts,), jnp.float32, smallest / len(split), largest / len(split))
        return jnp.repeat(jnp.exp(heights), dims[dim] // parts).reshape((-1,) + (1,) * (len(dims) - dim - 1))

    level = one(*split[0])
    for cut in split[1:]:
        level = level * one(*cut)
    return level


def bell_draw(stream_key, shape, deviation, reach, split=(), held_as=jnp.bfloat16):
    entries = jax.random.normal(stream_key, shape, jnp.float32) * deviation
    if len(split) > 0:
        entries = levels(stream_key, shape, split, -0.22, 0.18) * entries
    return jnp.clip(entries, min=-reach, max=reach).astype(held_as)


def setup_inputs(seed: int = 0) -> dict:
    key_list = jax.random.split(jax.random.key(seed), 4)
    return {
        "grads": bell_draw(key_list[0], (EXAMPLES, P_SIZE), (P_SIZE ** -0.25), 0.44595265, ((0, 16), (1, 16)), jnp.float32),
        "resid": jnp.clip(jnp.exp(math.log(1.0) - 2.3025851 * jax.random.uniform(key_list[1], (EXAMPLES,), jnp.float32) ** levels(key_list[1], (EXAMPLES,), ((0, 16),), -0.2, 0.2)), 0.1, 1.0),
        "offsets": jax.random.randint(key_list[2], (STEPS,), 0, RES_DEV - GROUP + 1).astype(jnp.int32),
    }


def reference(grads, resid, offsets):
    shards = grads.reshape(N_EX, RES_DEV, P_SIZE)
    weights = resid.reshape(N_EX, RES_DEV)
    results = []
    for step in range(STEPS):
        source = jnp.roll(shards, step + 1, axis=0)
        source_w = jnp.roll(weights, step + 1, axis=0)
        start = offsets[step].astype(jnp.int32)
        block = lax.dynamic_slice_in_dim(source, start, GROUP, 1)
        block_w = lax.dynamic_slice_in_dim(source_w, start, GROUP, 1)
        dots = jnp.einsum("ecp,erp->cer", block, shards, precision=lax.Precision.HIGHEST)
        tile = dots * dots * jnp.transpose(block_w)[:, :, None] * weights[None, :, :]
        results.append(tile.reshape(GROUP, EXAMPLES))
    return jnp.stack(results)
```

```python
import functools

import jax
import jax.numpy as jnp
from jax import lax
from jax.experimental import pallas as pl
from jax.experimental.pallas import tpu as pltpu
from jax.sharding import PartitionSpec as P

GROUP = 512
STEPS = 3
CHUNKS = 8
QUARTERS = 4
MESH = pl.DeviceIdType.MESH


def product(left, right):
    return lax.dot_general(
        left,
        right,
        (((1,), (1,)), ((), ())),
        precision=lax.Precision.HIGH,
        preferred_element_type=jnp.float32,
    )


def kernel(
    grads, near, mid, far, resid, out,
    near_v, mid_far_v, mid_v, far_v, far_far_v, res_v, res_far_v,
    part, parts_in, total, back_near, back_far,
    res_send, res_recv, relay_send, relay_recv, vis_send, vis_recv, cut_send, cut_recv,
    sum_send, sum_recv, ret_send, ret_recv, load_sem,
):
    n_ex, n_feat = lax.axis_size("ex"), lax.axis_size("feat")
    ex, feat = lax.axis_index("ex"), lax.axis_index("feat")
    rows = res_v.shape[1]
    wide = mid_v.shape[2]
    depth = grads.shape[1]
    narrow = depth - wide
    own = near.shape[1]
    quarter = own // QUARTERS
    owners = n_feat // QUARTERS

    def along(step):
        return {"ex": lax.rem(ex + step + n_ex, n_ex)}

    def across(step):
        return {"feat": lax.rem(feat + step, n_feat)}

    def remote(src, dst, send, recv, device):
        return pltpu.make_async_remote_copy(
            src_ref=src, dst_ref=dst, send_sem=send, recv_sem=recv, device_id=device, device_id_type=MESH
        )

    def residents(chunk):
        return remote(
            grads.at[pl.ds(pl.multiple_of(chunk * rows, rows), rows), :],
            res_v.at[chunk], res_send.at[chunk], res_recv.at[chunk], along(-1),
        )

    def relay(chunk):
        return remote(
            res_v.at[chunk, :, pl.ds(wide, narrow)],
            res_far_v.at[chunk], relay_send.at[chunk], relay_recv.at[chunk], along(-1),
        )

    def mid_visit(chunk):
        some = pl.ds(chunk * owners, owners)
        return remote(
            mid.at[some, :, pl.ds(0, wide)], mid_v.at[some], vis_send.at[chunk], vis_recv.at[chunk], along(1)
        )

    def far_cut_visit(chunk):
        some = pl.ds(chunk * owners, owners)
        return remote(
            far.at[some, :, pl.ds(wide, narrow)], far_far_v.at[some], cut_send.at[chunk], cut_recv.at[chunk], along(1)
        )

    def far_visit(chunk):
        q = chunk - QUARTERS
        return remote(
            far.at[:, pl.ds(pl.multiple_of(q * quarter, quarter), quarter), pl.ds(0, wide)],
            far_v.at[q], vis_send.at[chunk], vis_recv.at[chunk], along(2),
        )

    def start_visit(chunk):
        @pl.when(chunk < QUARTERS)
        def _():
            mid_visit(chunk).start()
            far_cut_visit(chunk).start()

        @pl.when(jnp.logical_and(chunk >= QUARTERS, chunk < 2 * QUARTERS))
        def _():
            far_visit(chunk).start()

    def columns(chunk):
        return pl.ds(pl.multiple_of(chunk * rows, rows), rows)

    def near_unit(c):
        return c, pl.ds(0, 1), pl.ds(0, own), columns(c), rows

    def mid_unit(c):
        return CHUNKS + c, pl.ds(1, 1), pl.ds(0, own), columns(c), rows

    def cut_unit(c):
        return 2 * CHUNKS + c, pl.ds(STEPS, 2), pl.ds(0, own), columns(c), rows

    last = (CHUNKS - 1) * rows
    upper = own - quarter
    far_units = (
        (3 * CHUNKS, pl.ds(2, 1), pl.ds(0, upper), pl.ds(0, last)),
        (3 * CHUNKS + 1, pl.ds(2, 1), pl.ds(upper, quarter), pl.ds(0, last)),
        (3 * CHUNKS + 2, pl.ds(2, 1), pl.ds(0, own), pl.ds(last, rows)),
    )

    def send_unit(unit):
        sem, tiles, lines, cols = unit[:4]

        @pl.loop(1, n_feat)
        def _(k):
            remote(
                part.at[lax.rem(feat + k, n_feat), tiles, lines, cols],
                parts_in.at[k - 1, tiles, lines, cols],
                sum_send.at[sem], sum_recv.at[sem], across(k),
            ).start()

    def all_parts(unit):
        sem, tiles, lines, cols = unit[:4]
        return remote(
            part.at[pl.ds(0, n_feat - 1), tiles, lines, cols],
            parts_in.at[:, tiles, lines, cols],
            sum_send.at[sem], sum_recv.at[sem], across(1),
        )

    def finish_unit(unit, far_home):
        _, tiles, lines, cols = unit[:4]
        all_parts(unit).wait_recv()
        value = part[feat, tiles, lines, cols]
        for k in range(n_feat - 1):
            value = value + parts_in[k, tiles, lines, cols]
        total[tiles, lines, cols] = value
        if far_home:
            remote(
                total.at[tiles, lines, cols], back_far.at[:, lines, cols], ret_send.at[1], ret_recv.at[1], along(2)
            ).start()
        else:
            remote(
                total.at[tiles, lines, cols], back_near.at[tiles, lines, cols], ret_send.at[0], ret_recv.at[0], along(1)
            ).start()

    barrier = pltpu.get_barrier_semaphore()
    for step in (-2, -1, 1, 2):
        pl.semaphore_signal(barrier, inc=1, device_id=along(step), device_id_type=MESH)

    @pl.loop(1, n_feat)
    def _(k):
        pl.semaphore_signal(barrier, inc=1, device_id=across(k), device_id_type=MESH)

    pl.semaphore_wait(barrier, 4 + n_feat - 1)

    for chunk in range(2):
        residents(chunk).start()
        mid_visit(chunk).start()
        far_cut_visit(chunk).start()
    loads = (
        pltpu.make_async_copy(near, near_v, load_sem.at[0]),
        pltpu.make_async_copy(mid.at[:, :, pl.ds(wide, narrow)], mid_far_v, load_sem.at[1]),
    )
    for load in loads:
        load.start()
    for load in loads:
        load.wait()

    def whole(ref):
        return ref[...].reshape(n_feat * own, ref.shape[2])

    def spread(value, height):
        return value.reshape(n_feat, height, rows)

    @pl.loop(0, CHUNKS)
    def _(t):
        residents(t).wait_recv()
        relay(t).start()
        residents(t).wait_send()

        @pl.when(t + 2 < CHUNKS)
        def _():
            residents(t + 2).start()

        part[:, 0, :, columns(t)] = spread(product(whole(near_v), res_v[t]), own)
        send_unit(near_unit(t))

        @pl.when(t < QUARTERS)
        def _():
            mid_visit(t).wait_recv()
            far_cut_visit(t).wait_recv()
            start_visit(t + 2)

        mid_first = jnp.where(t < QUARTERS - 1, t + 1, jnp.where(t == QUARTERS - 1, 0, t))

        @pl.loop(mid_first, t + 1)
        def _(c):
            part[:, 1, :, columns(c)] = spread(product(whole(mid_v), res_v[c, :, pl.ds(0, wide)]), own)
            send_unit(mid_unit(c))

        cut_first = jnp.where(t == QUARTERS, 0, t - 1)
        cut_end = jnp.where(t < QUARTERS, cut_first, jnp.where(t == CHUNKS - 1, CHUNKS, t))

        @pl.loop(cut_first, cut_end)
        def _(c):
            relay(c).wait_recv()
            block = res_far_v[c]
            part[:, STEPS, :, columns(c)] = spread(product(whole(mid_far_v), block), own)
            part[:, STEPS + 1, :, columns(c)] = spread(product(whole(far_far_v), block), own)
            send_unit(cut_unit(c))

        @pl.when(t > 0)
        def _():
            finish_unit(near_unit(t - 1), False)

        done_first = jnp.where(t == QUARTERS, 0, t - 1)
        done_end = jnp.where(t < QUARTERS, done_first, t)

        @pl.loop(done_first, done_end)
        def _(c):
            finish_unit(mid_unit(c), False)

        cut_done_first = jnp.where(t == QUARTERS + 1, 0, t - 2)
        cut_done_end = jnp.where(t < QUARTERS + 1, cut_done_first, t - 1)

        @pl.loop(cut_done_first, cut_done_end)
        def _(c):
            finish_unit(cut_unit(c), True)

        @pl.when(t >= QUARTERS)
        def _():
            far_visit(t).wait_recv()
            start_visit(t + 2)
            q = t - QUARTERS

            def piece(q, c):
                lines = pl.ds(pl.multiple_of(q * quarter, quarter), quarter)
                value = product(
                    far_v[q].reshape(n_feat * quarter, wide), res_v[c, :, pl.ds(0, wide)]
                )
                part[:, 2, lines, columns(c)] = spread(value, quarter)

            @pl.loop(0, t + q + 1)
            def _(i):
                earlier = i < t
                piece(jnp.where(earlier, q, i - t), jnp.where(earlier, i, t))

            @pl.when(t == CHUNKS - 2)
            def _():
                send_unit(far_units[0])

            @pl.when(t == CHUNKS - 1)
            def _():
                send_unit(far_units[1])
                send_unit(far_units[2])

    finish_unit(near_unit(CHUNKS - 1), False)
    finish_unit(mid_unit(CHUNKS - 1), False)
    for c in (CHUNKS - 2, CHUNKS - 1):
        finish_unit(cut_unit(c), True)
    for unit in far_units:
        finish_unit(unit, False)

    remote(total.at[pl.ds(0, STEPS)], back_near, ret_send.at[0], ret_recv.at[0], along(1)).wait()
    remote(total.at[pl.ds(STEPS, 2)], back_far, ret_send.at[1], ret_recv.at[1], along(2)).wait()
    weight = resid[...]
    dots = back_near[0]
    out[0] = dots * dots * weight
    for step in (1, 2):
        dots = back_near[step] + back_far[step - 1]
        out[step] = dots * dots * weight

    @pl.loop(0, CHUNKS)
    def _(t):
        relay(t).wait_send()
        all_parts(near_unit(t)).wait_send()
        all_parts(mid_unit(t)).wait_send()
        all_parts(cut_unit(t)).wait_send()

    for unit in far_units:
        all_parts(unit).wait_send()

    @pl.loop(0, QUARTERS)
    def _(t):
        mid_visit(t).wait_send()
        far_cut_visit(t).wait_send()
        far_visit(t + QUARTERS).wait_send()


def shards(grads, resid, offsets):
    n_feat = lax.axis_size("feat")
    count, depth = grads.shape
    own = GROUP // n_feat
    rows = count // CHUNKS
    narrow = depth // 4
    wide = depth - narrow
    scale = jnp.sqrt(resid)
    blocks = []
    for step in range(STEPS):
        start = offsets[step]
        block = lax.dynamic_slice_in_dim(grads, start, GROUP, 0)
        block_scale = lax.dynamic_slice_in_dim(scale, start, GROUP, 0)
        blocks.append((block * block_scale[:, None]).reshape(n_feat, own, depth))
    f32 = jnp.float32
    units = 3 * CHUNKS + 3
    dma = pltpu.SemaphoreType.DMA
    return pl.pallas_call(
        kernel,
        out_shape=jax.ShapeDtypeStruct((STEPS, own, count), f32),
        in_specs=[pl.BlockSpec(memory_space=pl.ANY)] * 4 + [pl.BlockSpec(memory_space=pltpu.VMEM)],
        out_specs=pl.BlockSpec(memory_space=pltpu.VMEM),
        scratch_shapes=[
            pltpu.VMEM((n_feat, own, depth), f32),
            pltpu.VMEM((n_feat, own, narrow), f32),
            pltpu.VMEM((n_feat, own, wide), f32),
            pltpu.VMEM((QUARTERS, n_feat, own // QUARTERS, wide), f32),
            pltpu.VMEM((n_feat, own, narrow), f32),
            pltpu.VMEM((CHUNKS, rows, depth), f32),
            pltpu.VMEM((CHUNKS, rows, narrow), f32),
            pltpu.VMEM((n_feat, STEPS + 2, own, count), f32),
            pltpu.VMEM((n_feat - 1, STEPS + 2, own, count), f32),
            pltpu.VMEM((STEPS + 2, own, count), f32),
            pltpu.VMEM((STEPS, own, count), f32),
            pltpu.VMEM((2, own, count), f32),
            dma((CHUNKS,)), dma((CHUNKS,)), dma((CHUNKS,)), dma((CHUNKS,)),
            dma((CHUNKS,)), dma((CHUNKS,)), dma((QUARTERS,)), dma((QUARTERS,)),
            dma((units,)), dma((units,)), dma((2,)), dma((2,)), dma((2,)),
        ],
        compiler_params=pltpu.CompilerParams(
            collective_id=0, has_side_effects=True, vmem_limit_bytes=60 * 2**20
        ),
    )(grads, *blocks, resid[None, :])


def solution(mesh):
    return jax.shard_map(
        shards,
        mesh=mesh,
        in_specs=(P("ex", "feat"), P("ex"), P()),
        out_specs=P(None, "feat", "ex"),
        check_vma=False,
    )
```

```python
import functools

import jax
import jax.numpy as jnp
from jax import lax
from jax.experimental import pallas as pl
from jax.experimental.pallas import tpu as pltpu
from jax.sharding import PartitionSpec as P

GROUP = 512
STEPS = 3
CHUNKS = 8
AHEAD = 3
QUARTERS = 4
HALF = CHUNKS // 2
MESH = pl.DeviceIdType.MESH


def product(left, right):
    return lax.dot_general(
        left,
        right,
        (((1,), (1,)), ((), ())),
        precision=lax.Precision.HIGH,
        preferred_element_type=jnp.float32,
    )


def kernel(
    grads, near, mid, far, resid, out,
    near_v, mid_far_v, mid_v, far_v, far_far_v, res_v, res_far_v,
    part, core_in, row_in, pair_in, total, back_near, back_far,
    far_part, far_core_in, far_row_in, far_pair_in, far_total, far_back,
    res_send, res_recv, relay_send, relay_recv, vis_send, vis_recv, cut_send, cut_recv,
    core_send, core_recv, row_send, row_recv, pair_send, pair_recv, ret_send, ret_recv, load_sem,
):
    n_ex, n_feat = lax.axis_size("ex"), lax.axis_size("feat")
    ex, feat = lax.axis_index("ex"), lax.axis_index("feat")
    rows = res_v.shape[1]
    wide = mid_v.shape[2]
    depth = grads.shape[1]
    narrow = depth - wide
    own = near.shape[1]
    quarter = own // QUARTERS
    owners = n_feat // QUARTERS
    n_row = n_feat // 4
    row, pair, core = feat // 4, lax.rem(feat // 2, 2), lax.rem(feat, 2)

    def along(step):
        return {"ex": lax.rem(ex + step + n_ex, n_ex)}

    def other_core():
        return {"feat": feat + 1 - 2 * core}

    def in_row(step):
        return {"feat": lax.rem(row + step, n_row) * 4 + lax.rem(feat, 4)}

    def other_pair():
        return {"feat": feat + 2 - 4 * pair}

    def remote(src, dst, send, recv, device):
        return pltpu.make_async_remote_copy(
            src_ref=src, dst_ref=dst, send_sem=send, recv_sem=recv, device_id=device, device_id_type=MESH
        )

    def residents(chunk):
        return remote(
            grads.at[pl.ds(pl.multiple_of(chunk * rows, rows), rows), :],
            res_v.at[chunk], res_send.at[chunk], res_recv.at[chunk], along(-1),
        )

    def relay(chunk):
        return remote(
            res_v.at[chunk, :, pl.ds(wide, narrow)],
            res_far_v.at[chunk], relay_send.at[chunk], relay_recv.at[chunk], along(-1),
        )

    def mid_visit(chunk):
        some = pl.ds(chunk * owners, owners)
        return remote(
            mid.at[some, :, pl.ds(0, wide)], mid_v.at[some], vis_send.at[chunk], vis_recv.at[chunk], along(1)
        )

    def far_cut_visit(chunk):
        some = pl.ds(chunk * owners, owners)
        return remote(
            far.at[some, :, pl.ds(wide, narrow)], far_far_v.at[some], cut_send.at[chunk], cut_recv.at[chunk], along(1)
        )

    def far_visit(chunk):
        q = chunk - QUARTERS
        return remote(
            far.at[:, pl.ds(pl.multiple_of(q * quarter, quarter), quarter), pl.ds(0, wide)],
            far_v.at[q], vis_send.at[chunk], vis_recv.at[chunk], along(2),
        )

    def start_visit(chunk):
        @pl.when(chunk < QUARTERS)
        def _():
            mid_visit(chunk).start()
            far_cut_visit(chunk).start()

        @pl.when(jnp.logical_and(chunk >= QUARTERS, chunk < 2 * QUARTERS))
        def _():
            far_visit(chunk).start()

    def near_unit(c):
        return c, False, pl.ds(0, 1), pl.ds(c, 1)

    def whole_unit(c):
        return c, False, pl.ds(0, 4), pl.ds(c, 1)

    first_unit = (CHUNKS, False, pl.ds(1, 3), pl.ds(0, HALF))
    far_units = (
        (CHUNKS + 1, True, pl.ds(0, QUARTERS - 1), pl.ds(0, CHUNKS - 1)),
        (CHUNKS + 2, True, pl.ds(0, QUARTERS - 1), pl.ds(CHUNKS - 1, 1)),
        (CHUNKS + 3, True, pl.ds(QUARTERS - 1, 1), pl.ds(0, CHUNKS)),
    )

    def own_part(unit, c, x, y):
        _, far, i, j = unit
        return (far_part, (c, x, y, i, j)) if far else (part, (c, i, j, x, y))

    def from_core(unit, x):
        _, far, i, j = unit
        return (far_core_in, (x, slice(None), i, j)) if far else (core_in, (i, j, x))

    def from_row(unit, k):
        _, far, i, j = unit
        return (far_row_in, (k, slice(None), i, j)) if far else (row_in, (k, i, j))

    def from_pair(unit):
        _, far, i, j = unit
        return (far_pair_in, (i, j)) if far else (pair_in, (i, j))

    def at(place):
        return place[0].at[place[1]]

    def read(place):
        return place[0][place[1]]

    every = slice(None)

    def core_copy(unit):
        sem = unit[0]
        return remote(
            at(own_part(unit, 1 - core, every, every)), at(from_core(unit, every)),
            core_send.at[sem], core_recv.at[sem], other_core(),
        )

    def row_copy(unit, step):
        sem = unit[0]
        return remote(
            at(own_part(unit, core, lax.rem(row + step, n_row), every)), at(from_row(unit, step - 1)),
            row_send.at[sem], row_recv.at[sem], in_row(step),
        )

    def row_copies(unit):
        sem = unit[0]
        block = at(from_row(unit, every))
        return remote(block, block, row_send.at[sem], row_recv.at[sem], in_row(1))

    def pair_copy(unit):
        sem = unit[0]
        return remote(
            at(own_part(unit, core, row, 1 - pair)), at(from_pair(unit)),
            pair_send.at[sem], pair_recv.at[sem], other_pair(),
        )

    def start_sum(unit):
        core_copy(unit).start()

    def sum_cores(unit):
        core_copy(unit).wait_recv()

        @pl.loop(0, n_row)
        def _(x):
            ref, index = own_part(unit, core, x, every)
            ref[index] = ref[index] + read(from_core(unit, x))

        for step in range(1, n_row):
            row_copy(unit, step).start()

    def sum_row(unit):
        row_copies(unit).wait_recv()
        ref, index = own_part(unit, core, row, every)
        value = ref[index]
        for k in range(n_row - 1):
            value = value + read(from_row(unit, k))
        ref[index] = value
        pair_copy(unit).start()

    def send_back(src, dst, sem, step):
        remote(src, dst, ret_send.at[sem], ret_recv.at[sem], along(step)).start()

    def sum_pair(unit):
        pair_copy(unit).wait_recv()
        _, far, i, j = unit
        value = read(own_part(unit, core, row, pair)) + read(from_pair(unit))
        if far:
            far_total[i, j] = value
            send_back(far_total.at[i, j], far_back.at[i, j], 2, 1)
            return
        total[i, j] = value
        low, high = i.start, i.start + i.size
        near_home = pl.ds(low, min(high, 2) - low)
        send_back(total.at[near_home, j], back_near.at[near_home, j], 0, 1)
        if high > 2:
            send_back(total.at[pl.ds(2, 2), j], back_far.at[:, j], 1, 2)

    def wait_sum(unit):
        core_copy(unit).wait_send()
        row_copies(unit).wait_send()
        pair_copy(unit).wait_send()

    def advance(ready, stage):
        @pl.when(jnp.logical_and(ready >= 0, ready < HALF))
        def _():
            stage(near_unit(ready))

        @pl.when(ready == HALF - 1)
        def _():
            stage(first_unit)

        @pl.when(jnp.logical_and(ready >= HALF, ready < CHUNKS - 1))
        def _():
            stage(whole_unit(ready))

        @pl.when(ready == CHUNKS - 2)
        def _():
            stage(far_units[0])

    barrier = pltpu.get_barrier_semaphore()
    for step in (-2, -1, 1, 2):
        pl.semaphore_signal(barrier, inc=1, device_id=along(step), device_id_type=MESH)

    for device in (other_core(), other_pair()) + tuple(in_row(step) for step in range(1, n_row)):
        pl.semaphore_signal(barrier, inc=1, device_id=device, device_id_type=MESH)
    pl.semaphore_wait(barrier, 4 + 2 + n_row - 1)

    for chunk in range(AHEAD):
        residents(chunk).start()
        mid_visit(chunk).start()
        far_cut_visit(chunk).start()
    loads = (
        pltpu.make_async_copy(near, near_v, load_sem.at[0]),
        pltpu.make_async_copy(mid.at[:, :, pl.ds(wide, narrow)], mid_far_v, load_sem.at[1]),
    )
    for load in loads:
        load.start()
    for load in loads:
        load.wait()

    def whole(ref):
        return ref[...].reshape(n_feat * own, ref.shape[2])

    def keep(value, tile, c):
        value = value.reshape(n_row, 2, 2, own, rows)
        for k in range(2):
            part[k, tile, c] = value[:, :, k]

    def near_tile(c):
        keep(product(whole(near_v), res_v[c]), 0, c)

    def mid_tile(c):
        keep(product(whole(mid_v), res_v[c, :, pl.ds(0, wide)]), 1, c)

    def cut_tiles(c):
        relay(c).wait_recv()
        block = res_far_v[c]
        keep(product(whole(mid_far_v), block), 2, c)
        keep(product(whole(far_far_v), block), 3, c)

    def far_tile(q, c):
        value = product(far_v[q].reshape(n_feat * quarter, wide), res_v[c, :, pl.ds(0, wide)])
        value = value.reshape(n_row, 2, 2, quarter, rows)
        for k in range(2):
            far_part[k, :, :, q, c] = value[:, :, k]

    @pl.loop(0, CHUNKS - 1)
    def _(t):
        residents(t).wait_recv()
        relay(t).start()
        residents(t).wait_send()

        @pl.when(t + AHEAD < CHUNKS)
        def _():
            residents(t + AHEAD).start()

        near_tile(t)

        @pl.when(t < QUARTERS)
        def _():
            mid_visit(t).wait_recv()
            far_cut_visit(t).wait_recv()
            start_visit(t + AHEAD)

        @pl.loop(jnp.where(t < HALF - 1, t + 1, jnp.where(t == HALF - 1, 0, t)), t + 1)
        def _(c):
            mid_tile(c)

        @pl.when(t >= QUARTERS)
        def _():
            far_visit(t).wait_recv()
            start_visit(t + AHEAD)
            q = t - QUARTERS

            @pl.loop(0, t + q + 1)
            def _(i):
                earlier = i < t
                far_tile(jnp.where(earlier, q, i - t), jnp.where(earlier, i, t))

        @pl.loop(jnp.where(t < HALF - 1, t + 1, jnp.where(t == HALF - 1, 0, t)), t + 1)
        def _(c):
            cut_tiles(c)

        advance(t, start_sum)
        advance(t - 2, sum_row)
        advance(t - 1, sum_cores)

    end = CHUNKS - 1
    residents(end).wait_recv()
    relay(end).start()
    residents(end).wait_send()
    near_tile(end)
    mid_tile(end)
    advance(jnp.int32(end - 1), sum_cores)
    advance(jnp.int32(end - 2), sum_row)
    for q in range(QUARTERS - 1):
        far_tile(q, end)
    start_sum(far_units[1])
    cut_tiles(end)
    start_sum(whole_unit(end))
    advance(jnp.int32(end - 1), sum_row)
    for stage in (sum_cores, sum_row):
        stage(far_units[1])
        stage(whole_unit(end))

    @pl.loop(0, end)
    def _(ready):
        advance(ready, sum_pair)

    for unit in (far_units[1], whole_unit(end)):
        sum_pair(unit)
    far_visit(end).wait_recv()

    @pl.loop(0, CHUNKS)
    def _(c):
        far_tile(QUARTERS - 1, c)

    start_sum(far_units[2])
    for stage in (sum_cores, sum_row, sum_pair):
        stage(far_units[2])

    remote(total.at[pl.ds(0, 2)], back_near, ret_send.at[0], ret_recv.at[0], along(1)).wait()
    remote(total.at[pl.ds(2, 2)], back_far, ret_send.at[1], ret_recv.at[1], along(2)).wait()
    remote(far_total, far_back, ret_send.at[2], ret_recv.at[2], along(1)).wait()
    for c in range(CHUNKS):
        cols = pl.ds(c * rows, rows)
        weight = resid[:, cols]
        tiles = (
            back_near[0, c],
            back_near[1, c] + back_far[0, c],
            far_back[:, c].reshape(own, rows) + back_far[1, c],
        )
        for step, dots in enumerate(tiles):
            out[step, :, cols] = dots * dots * weight

    @pl.loop(0, CHUNKS)
    def _(t):
        relay(t).wait_send()

        @pl.when(t < HALF)
        def _():
            wait_sum(near_unit(t))

        @pl.when(t >= HALF)
        def _():
            wait_sum(whole_unit(t))

    for unit in (first_unit,) + far_units:
        wait_sum(unit)

    @pl.loop(0, QUARTERS)
    def _(t):
        mid_visit(t).wait_send()
        far_cut_visit(t).wait_send()
        far_visit(t + QUARTERS).wait_send()


def shards(grads, resid, offsets):
    n_feat = lax.axis_size("feat")
    count, depth = grads.shape
    own = GROUP // n_feat
    rows = count // CHUNKS
    narrow = depth // 4
    wide = depth - narrow
    scale = jnp.sqrt(resid)
    blocks = []
    for step in range(STEPS):
        start = offsets[step]
        block = lax.dynamic_slice_in_dim(grads, start, GROUP, 0)
        block_scale = lax.dynamic_slice_in_dim(scale, start, GROUP, 0)
        blocks.append((block * block_scale[:, None]).reshape(n_feat, own, depth))
    f32 = jnp.float32
    units = CHUNKS + 4
    dma = pltpu.SemaphoreType.DMA
    xs = n_feat // 4
    far = (QUARTERS, CHUNKS, own // QUARTERS, rows)
    return pl.pallas_call(
        kernel,
        out_shape=jax.ShapeDtypeStruct((STEPS, own, count), f32),
        in_specs=[pl.BlockSpec(memory_space=pl.ANY)] * 4 + [pl.BlockSpec(memory_space=pltpu.VMEM)],
        out_specs=pl.BlockSpec(memory_space=pltpu.VMEM),
        scratch_shapes=[
            pltpu.VMEM((n_feat, own, depth), f32),
            pltpu.VMEM((n_feat, own, narrow), f32),
            pltpu.VMEM((n_feat, own, wide), f32),
            pltpu.VMEM((QUARTERS, n_feat, own // QUARTERS, wide), f32),
            pltpu.VMEM((n_feat, own, narrow), f32),
            pltpu.VMEM((CHUNKS, rows, depth), f32),
            pltpu.VMEM((CHUNKS, rows, narrow), f32),
            pltpu.VMEM((2, 4, CHUNKS, xs, 2, own, rows), f32),
            pltpu.VMEM((4, CHUNKS, xs, 2, own, rows), f32),
            pltpu.VMEM((xs - 1, 4, CHUNKS, 2, own, rows), f32),
            pltpu.VMEM((4, CHUNKS, own, rows), f32),
            pltpu.VMEM((4, CHUNKS, own, rows), f32),
            pltpu.VMEM((2, CHUNKS, own, rows), f32),
            pltpu.VMEM((2, CHUNKS, own, rows), f32),
            pltpu.VMEM((2, xs, 2) + far, f32),
            pltpu.VMEM((xs, 2) + far, f32),
            pltpu.VMEM((xs - 1, 2) + far, f32),
            pltpu.VMEM(far, f32),
            pltpu.VMEM(far, f32),
            pltpu.VMEM(far, f32),
            dma((CHUNKS,)), dma((CHUNKS,)), dma((CHUNKS,)), dma((CHUNKS,)),
            dma((CHUNKS,)), dma((CHUNKS,)), dma((QUARTERS,)), dma((QUARTERS,)),
            dma((units,)), dma((units,)), dma((units,)), dma((units,)), dma((units,)), dma((units,)), dma((3,)), dma((3,)), dma((2,)),
        ],
        compiler_params=pltpu.CompilerParams(
            collective_id=0, has_side_effects=True, vmem_limit_bytes=60 * 2**20
        ),
    )(grads, *blocks, resid[None, :])


def solution(mesh):
    return jax.shard_map(
        shards,
        mesh=mesh,
        in_specs=(P("ex", "feat"), P("ex"), P()),
        out_specs=P(None, "feat", "ex"),
        check_vma=False,
    )
```

```python
import functools

import jax
import jax.numpy as jnp
from jax import lax
from jax.experimental import pallas as pl
from jax.experimental.pallas import tpu as pltpu
from jax.sharding import PartitionSpec as P

GROUP = 512
STEPS = 3
CHUNKS = 8
AHEAD = 2
QUARTERS = 4
HALF = CHUNKS // 2
PICKED = 512
MESH = pl.DeviceIdType.MESH


def product(left, right):
    return lax.dot_general(
        left,
        right,
        (((1,), (1,)), ((), ())),
        precision=lax.Precision.HIGH,
        preferred_element_type=jnp.float32,
    )


def kernel(
    offsets, grads, resid, out,
    grads_v, near_v, mid, far, mid_v, far_v, far_far_v, res_v, res_far_v,
    part, core_in, row_in, pair_in, total, back_near, back_far,
    far_part, far_core_in, far_row_in, far_pair_in, far_total, far_back,
    res_send, res_recv, relay_send, relay_recv, vis_send, vis_recv, cut_send, cut_recv,
    core_send, core_recv, row_send, row_recv, pair_send, pair_recv, ret_send, ret_recv, load_sem,
):
    n_ex, n_feat = lax.axis_size("ex"), lax.axis_size("feat")
    ex, feat = lax.axis_index("ex"), lax.axis_index("feat")
    rows = res_v.shape[1]
    wide = mid_v.shape[2]
    depth = grads.shape[1]
    narrow = depth - wide
    own = near_v.shape[1]
    quarter = own // QUARTERS
    owners = n_feat // QUARTERS
    n_row = n_feat // 4
    row, pair, core = feat // 4, lax.rem(feat // 2, 2), lax.rem(feat, 2)

    def along(step):
        return {"ex": lax.rem(ex + step + n_ex, n_ex)}

    def other_core():
        return {"feat": feat + 1 - 2 * core}

    def in_row(step):
        return {"feat": lax.rem(row + step, n_row) * 4 + lax.rem(feat, 4)}

    def other_pair():
        return {"feat": feat + 2 - 4 * pair}

    def remote(src, dst, send, recv, device):
        return pltpu.make_async_remote_copy(
            src_ref=src, dst_ref=dst, send_sem=send, recv_sem=recv, device_id=device, device_id_type=MESH
        )

    def residents(chunk):
        return remote(
            grads.at[pl.ds(pl.multiple_of(chunk * rows, rows), rows), :],
            res_v.at[chunk], res_send.at[chunk], res_recv.at[chunk], along(-1),
        )

    def relay(chunk):
        return remote(
            res_v.at[chunk, :, pl.ds(wide, narrow)],
            res_far_v.at[chunk], relay_send.at[chunk], relay_recv.at[chunk], along(-1),
        )

    def mid_visit(chunk):
        some = pl.ds(chunk * owners, owners)
        return remote(
            mid.at[some, :, pl.ds(0, wide)], mid_v.at[some], vis_send.at[chunk], vis_recv.at[chunk], along(1)
        )

    def far_cut_visit(chunk):
        some = pl.ds(chunk * owners, owners)
        return remote(
            far.at[some, :, pl.ds(wide, narrow)], far_far_v.at[some], cut_send.at[chunk], cut_recv.at[chunk], along(1)
        )

    def far_visit(chunk):
        q = chunk - QUARTERS
        return remote(
            far.at[:, pl.ds(pl.multiple_of(q * quarter, quarter), quarter), pl.ds(0, wide)],
            far_v.at[q], vis_send.at[chunk], vis_recv.at[chunk], along(2),
        )

    def start_visit(chunk):
        @pl.when(chunk < QUARTERS)
        def _():
            mid_visit(chunk).start()
            far_cut_visit(chunk).start()

        @pl.when(jnp.logical_and(chunk >= QUARTERS, chunk < 2 * QUARTERS))
        def _():
            far_visit(chunk).start()

    def near_unit(c):
        return c, False, pl.ds(0, 1), pl.ds(c, 1)

    def whole_unit(c):
        return c, False, pl.ds(0, 4), pl.ds(c, 1)

    first_unit = (CHUNKS, False, pl.ds(1, 3), pl.ds(0, HALF))
    far_units = (
        (CHUNKS + 1, True, pl.ds(0, QUARTERS - 1), pl.ds(0, CHUNKS - 1)),
        (CHUNKS + 2, True, pl.ds(0, QUARTERS - 1), pl.ds(CHUNKS - 1, 1)),
        (CHUNKS + 3, True, pl.ds(QUARTERS - 1, 1), pl.ds(0, CHUNKS)),
    )

    def own_part(unit, c, x, y):
        _, far, i, j = unit
        return (far_part, (c, x, y, i, j)) if far else (part, (c, i, j, x, y))

    def from_core(unit, x):
        _, far, i, j = unit
        return (far_core_in, (x, slice(None), i, j)) if far else (core_in, (i, j, x))

    def from_row(unit, k):
        _, far, i, j = unit
        return (far_row_in, (k, slice(None), i, j)) if far else (row_in, (k, i, j))

    def from_pair(unit):
        _, far, i, j = unit
        return (far_pair_in, (i, j)) if far else (pair_in, (i, j))

    def at(place):
        return place[0].at[place[1]]

    def read(place):
        return place[0][place[1]]

    every = slice(None)

    def core_copy(unit):
        sem = unit[0]
        return remote(
            at(own_part(unit, 1 - core, every, every)), at(from_core(unit, every)),
            core_send.at[sem], core_recv.at[sem], other_core(),
        )

    def row_copy(unit, step):
        sem = unit[0]
        return remote(
            at(own_part(unit, core, lax.rem(row + step, n_row), every)), at(from_row(unit, step - 1)),
            row_send.at[sem], row_recv.at[sem], in_row(step),
        )

    def row_copies(unit):
        sem = unit[0]
        block = at(from_row(unit, every))
        return remote(block, block, row_send.at[sem], row_recv.at[sem], in_row(1))

    def pair_copy(unit):
        sem = unit[0]
        return remote(
            at(own_part(unit, core, row, 1 - pair)), at(from_pair(unit)),
            pair_send.at[sem], pair_recv.at[sem], other_pair(),
        )

    def start_sum(unit):
        core_copy(unit).start()

    def sum_cores(unit):
        core_copy(unit).wait_recv()

        @pl.loop(0, n_row)
        def _(x):
            ref, index = own_part(unit, core, x, every)
            ref[index] = ref[index] + read(from_core(unit, x))

        for step in range(1, n_row):
            row_copy(unit, step).start()

    def sum_row(unit):
        row_copies(unit).wait_recv()
        ref, index = own_part(unit, core, row, every)
        value = ref[index]
        for k in range(n_row - 1):
            value = value + read(from_row(unit, k))
        ref[index] = value
        pair_copy(unit).start()

    def send_back(src, dst, sem, step):
        remote(src, dst, ret_send.at[sem], ret_recv.at[sem], along(step)).start()

    def sum_pair(unit):
        pair_copy(unit).wait_recv()
        _, far, i, j = unit
        value = read(own_part(unit, core, row, pair)) + read(from_pair(unit))
        if far:
            far_total[i, j] = value
            send_back(far_total.at[i, j], far_back.at[i, j], 2, 1)
            return
        total[i, j] = value
        low, high = i.start, i.start + i.size
        near_home = pl.ds(low, min(high, 2) - low)
        send_back(total.at[near_home, j], back_near.at[near_home, j], 0, 1)
        if high > 2:
            send_back(total.at[pl.ds(2, 2), j], back_far.at[:, j], 1, 2)

    def wait_sum(unit):
        core_copy(unit).wait_send()
        row_copies(unit).wait_send()
        pair_copy(unit).wait_send()

    def advance(ready, stage):
        @pl.when(jnp.logical_and(ready >= 0, ready < HALF))
        def _():
            stage(near_unit(ready))

        @pl.when(ready == HALF - 1)
        def _():
            stage(first_unit)

        @pl.when(jnp.logical_and(ready >= HALF, ready < CHUNKS - 1))
        def _():
            stage(whole_unit(ready))

        @pl.when(ready == CHUNKS - 2)
        def _():
            stage(far_units[0])

    barrier = pltpu.get_barrier_semaphore()
    for step in (-2, -1, 1, 2):
        pl.semaphore_signal(barrier, inc=1, device_id=along(step), device_id_type=MESH)

    for device in (other_core(), other_pair()) + tuple(in_row(step) for step in range(1, n_row)):
        pl.semaphore_signal(barrier, inc=1, device_id=device, device_id_type=MESH)
    pl.semaphore_wait(barrier, 4 + 2 + n_row - 1)

    for chunk in range(AHEAD):
        residents(chunk).start()
    load = pltpu.make_async_copy(grads, grads_v, load_sem)
    load.start()
    load.wait()

    count = grads_v.shape[0]
    some_rows = owners * own

    def take(step, block, chunk):
        line = lax.broadcasted_iota(jnp.int32, (some_rows, count), 0) + (offsets[step] + chunk * some_rows)
        source = lax.broadcasted_iota(jnp.int32, (some_rows, count), 1)
        pick = jnp.where(line == source, jnp.sqrt(resid[...]), 0.0)

        @pl.loop(0, depth // PICKED)
        def _(i):
            cols = pl.ds(pl.multiple_of(i * PICKED, PICKED), PICKED)
            value = lax.dot_general(
                pick,
                grads_v[:, cols],
                (((1,), (0,)), ((), ())),
                precision=lax.Precision.HIGH,
                preferred_element_type=jnp.float32,
            )
            block[pl.ds(chunk * owners, owners), :, cols] = value.reshape(owners, own, PICKED)

    @pl.loop(0, AHEAD)
    def _(chunk):
        take(1, mid, chunk)
        take(2, far, chunk)
        mid_visit(chunk).start()
        far_cut_visit(chunk).start()

    @pl.loop(0, QUARTERS)
    def _(chunk):
        take(0, near_v, chunk)

    def whole(ref):
        return ref[...].reshape(n_feat * own, ref.shape[2])

    def keep(value, tile, c):
        value = value.reshape(n_row, 2, 2, own, rows)
        for k in range(2):
            part[k, tile, c] = value[:, :, k]

    def near_tile(c):
        keep(product(whole(near_v), res_v[c]), 0, c)

    def mid_tile(c):
        keep(product(whole(mid_v), res_v[c, :, pl.ds(0, wide)]), 1, c)

    def cut_tiles(c):
        relay(c).wait_recv()
        block = res_far_v[c]
        keep(product(mid[:, :, pl.ds(wide, narrow)].reshape(n_feat * own, narrow), block), 2, c)
        keep(product(whole(far_far_v), block), 3, c)

    def far_tile(q, c):
        value = product(far_v[q].reshape(n_feat * quarter, wide), res_v[c, :, pl.ds(0, wide)])
        value = value.reshape(n_row, 2, 2, quarter, rows)
        for k in range(2):
            far_part[k, :, :, q, c] = value[:, :, k]

    @pl.loop(0, CHUNKS - 1)
    def _(t):
        residents(t).wait_recv()
        relay(t).start()
        residents(t).wait_send()

        @pl.when(t + AHEAD < CHUNKS)
        def _():
            residents(t + AHEAD).start()

        near_tile(t)

        @pl.when(t < QUARTERS)
        def _():
            mid_visit(t).wait_recv()
            far_cut_visit(t).wait_recv()

            @pl.when(t + AHEAD < QUARTERS)
            def _():
                take(1, mid, t + AHEAD)
                take(2, far, t + AHEAD)

            start_visit(t + AHEAD)

        @pl.loop(jnp.where(t < HALF - 1, t + 1, jnp.where(t == HALF - 1, 0, t)), t + 1)
        def _(c):
            mid_tile(c)

        @pl.when(t >= QUARTERS)
        def _():
            far_visit(t).wait_recv()
            start_visit(t + AHEAD)
            q = t - QUARTERS

            @pl.loop(0, t + q + 1)
            def _(i):
                earlier = i < t
                far_tile(jnp.where(earlier, q, i - t), jnp.where(earlier, i, t))

        @pl.loop(jnp.where(t < HALF - 1, t + 1, jnp.where(t == HALF - 1, 0, t)), t + 1)
        def _(c):
            cut_tiles(c)

        advance(t, start_sum)
        advance(t - 2, sum_row)
        advance(t - 1, sum_cores)

    end = CHUNKS - 1
    residents(end).wait_recv()
    relay(end).start()
    residents(end).wait_send()
    near_tile(end)
    mid_tile(end)
    advance(jnp.int32(end - 1), sum_cores)
    advance(jnp.int32(end - 2), sum_row)

    @pl.loop(0, end - 2)
    def _(ready):
        advance(ready, sum_pair)

    for q in range(QUARTERS - 1):
        far_tile(q, end)
    start_sum(far_units[1])
    cut_tiles(end)
    start_sum(whole_unit(end))
    advance(jnp.int32(end - 1), sum_row)
    for stage in (sum_cores, sum_row):
        stage(far_units[1])
        stage(whole_unit(end))

    @pl.loop(end - 2, end)
    def _(ready):
        advance(ready, sum_pair)

    for unit in (far_units[1], whole_unit(end)):
        sum_pair(unit)
    far_visit(end).wait_recv()

    @pl.loop(0, CHUNKS)
    def _(c):
        far_tile(QUARTERS - 1, c)

    start_sum(far_units[2])
    for stage in (sum_cores, sum_row, sum_pair):
        stage(far_units[2])

    remote(total.at[pl.ds(0, 2)], back_near, ret_send.at[0], ret_recv.at[0], along(1)).wait()
    remote(total.at[pl.ds(2, 2)], back_far, ret_send.at[1], ret_recv.at[1], along(2)).wait()
    remote(far_total, far_back, ret_send.at[2], ret_recv.at[2], along(1)).wait()
    for c in range(CHUNKS):
        cols = pl.ds(c * rows, rows)
        weight = resid[:, cols]
        tiles = (
            back_near[0, c],
            back_near[1, c] + back_far[0, c],
            far_back[:, c].reshape(own, rows) + back_far[1, c],
        )
        for step, dots in enumerate(tiles):
            out[step, :, cols] = dots * dots * weight

    @pl.loop(0, CHUNKS)
    def _(t):
        relay(t).wait_send()

        @pl.when(t < HALF)
        def _():
            wait_sum(near_unit(t))

        @pl.when(t >= HALF)
        def _():
            wait_sum(whole_unit(t))

    for unit in (first_unit,) + far_units:
        wait_sum(unit)

    @pl.loop(0, QUARTERS)
    def _(t):
        mid_visit(t).wait_send()
        far_cut_visit(t).wait_send()
        far_visit(t + QUARTERS).wait_send()


def shards(grads, resid, offsets):
    n_feat = lax.axis_size("feat")
    count, depth = grads.shape
    own = GROUP // n_feat
    rows = count // CHUNKS
    narrow = depth // 4
    wide = depth - narrow
    f32 = jnp.float32
    units = CHUNKS + 4
    dma = pltpu.SemaphoreType.DMA
    xs = n_feat // 4
    far = (QUARTERS, CHUNKS, own // QUARTERS, rows)
    return pl.pallas_call(
        kernel,
        out_shape=jax.ShapeDtypeStruct((STEPS, own, count), f32),
        in_specs=[
            pl.BlockSpec(memory_space=pltpu.SMEM),
            pl.BlockSpec(memory_space=pl.ANY),
            pl.BlockSpec(memory_space=pltpu.VMEM),
        ],
        out_specs=pl.BlockSpec(memory_space=pltpu.VMEM),
        scratch_shapes=[
            pltpu.VMEM((count, depth), f32),
            pltpu.VMEM((n_feat, own, depth), f32),
            pltpu.VMEM((n_feat, own, depth), f32),
            pltpu.VMEM((n_feat, own, depth), f32),
            pltpu.VMEM((n_feat, own, wide), f32),
            pltpu.VMEM((QUARTERS, n_feat, own // QUARTERS, wide), f32),
            pltpu.VMEM((n_feat, own, narrow), f32),
            pltpu.VMEM((CHUNKS, rows, depth), f32),
            pltpu.VMEM((CHUNKS, rows, narrow), f32),
            pltpu.VMEM((2, 4, CHUNKS, xs, 2, own, rows), f32),
            pltpu.VMEM((4, CHUNKS, xs, 2, own, rows), f32),
            pltpu.VMEM((xs - 1, 4, CHUNKS, 2, own, rows), f32),
            pltpu.VMEM((4, CHUNKS, own, rows), f32),
            pltpu.VMEM((4, CHUNKS, own, rows), f32),
            pltpu.VMEM((2, CHUNKS, own, rows), f32),
            pltpu.VMEM((2, CHUNKS, own, rows), f32),
            pltpu.VMEM((2, xs, 2) + far, f32),
            pltpu.VMEM((xs, 2) + far, f32),
            pltpu.VMEM((xs - 1, 2) + far, f32),
            pltpu.VMEM(far, f32),
            pltpu.VMEM(far, f32),
            pltpu.VMEM(far, f32),
            dma((CHUNKS,)), dma((CHUNKS,)), dma((CHUNKS,)), dma((CHUNKS,)),
            dma((CHUNKS,)), dma((CHUNKS,)), dma((QUARTERS,)), dma((QUARTERS,)),
            dma((units,)), dma((units,)), dma((units,)), dma((units,)), dma((units,)), dma((units,)), dma((3,)), dma((3,)), dma,
        ],
        compiler_params=pltpu.CompilerParams(
            collective_id=0, has_side_effects=True, vmem_limit_bytes=62 * 2**20
        ),
    )(offsets, grads, resid[None, :])


def solution(mesh):
    return jax.shard_map(
        shards,
        mesh=mesh,
        in_specs=(P("ex", "feat"), P("ex"), P()),
        out_specs=P(None, "feat", "ex"),
        check_vma=False,
    )
```

```python
import functools

import jax
import jax.numpy as jnp
from jax import lax
from jax.experimental import pallas as pl
from jax.experimental.pallas import tpu as pltpu
from jax.sharding import PartitionSpec as P

GROUP = 512
STEPS = 3
CHUNKS = 8
AHEAD = 2
QUARTERS = 4
HALF = CHUNKS // 2
PICKED = 512
MESH = pl.DeviceIdType.MESH


def product(left, right):
    return lax.dot_general(
        left,
        right,
        (((1,), (1,)), ((), ())),
        precision=lax.Precision.HIGH,
        preferred_element_type=jnp.float32,
    )


def kernel(
    offsets, grads, resid, out,
    grads_v, near_v, mid, far, mid_v, far_v, far_far_v, res_v, res_far_v,
    part, core_in, row_in, pair_in, total, back_near, back_far,
    far_part, far_core_in, far_row_in, far_pair_in, far_total, far_back,
    res_send, res_recv, relay_send, relay_recv, vis_send, vis_recv, cut_send, cut_recv,
    core_send, core_recv, row_send, row_recv, pair_send, pair_recv, ret_send, ret_recv, load_sem,
):
    n_ex, n_feat = lax.axis_size("ex"), lax.axis_size("feat")
    ex, feat = lax.axis_index("ex"), lax.axis_index("feat")
    rows = res_v.shape[1]
    wide = mid_v.shape[2]
    depth = grads.shape[1]
    narrow = depth - wide
    own = near_v.shape[1]
    quarter = own // QUARTERS
    owners = n_feat // QUARTERS
    n_row = n_feat // 4
    row, pair, core = feat // 4, lax.rem(feat // 2, 2), lax.rem(feat, 2)

    def along(step):
        return {"ex": lax.rem(ex + step + n_ex, n_ex)}

    def other_core():
        return {"feat": feat + 1 - 2 * core}

    def in_row(step):
        return {"feat": lax.rem(row + step, n_row) * 4 + lax.rem(feat, 4)}

    def other_pair():
        return {"feat": feat + 2 - 4 * pair}

    def remote(src, dst, send, recv, device):
        return pltpu.make_async_remote_copy(
            src_ref=src, dst_ref=dst, send_sem=send, recv_sem=recv, device_id=device, device_id_type=MESH
        )

    def residents(chunk):
        return remote(
            grads.at[pl.ds(pl.multiple_of(chunk * rows, rows), rows), :],
            res_v.at[chunk], res_send.at[chunk], res_recv.at[chunk], along(-1),
        )

    def relay(chunk):
        return remote(
            res_v.at[chunk, :, pl.ds(wide, narrow)],
            res_far_v.at[chunk], relay_send.at[chunk], relay_recv.at[chunk], along(-1),
        )

    def mid_visit(chunk):
        some = pl.ds(chunk * owners, owners)
        return remote(
            mid.at[some, :, pl.ds(0, wide)], mid_v.at[some], vis_send.at[chunk], vis_recv.at[chunk], along(1)
        )

    def far_cut_visit(chunk):
        some = pl.ds(chunk * owners, owners)
        return remote(
            far.at[some, :, pl.ds(wide, narrow)], far_far_v.at[some], cut_send.at[chunk], cut_recv.at[chunk], along(1)
        )

    def far_visit(chunk):
        q = chunk - QUARTERS
        return remote(
            far.at[:, pl.ds(pl.multiple_of(q * quarter, quarter), quarter), pl.ds(0, wide)],
            far_v.at[q], vis_send.at[chunk], vis_recv.at[chunk], along(2),
        )

    def start_visit(chunk):
        @pl.when(chunk < QUARTERS)
        def _():
            mid_visit(chunk).start()
            far_cut_visit(chunk).start()

        @pl.when(jnp.logical_and(chunk >= QUARTERS, chunk < 2 * QUARTERS))
        def _():
            far_visit(chunk).start()

    def near_unit(c):
        return c, False, pl.ds(0, 1), pl.ds(c, 1)

    def whole_unit(c):
        return c, False, pl.ds(0, 4), pl.ds(c, 1)

    first_unit = (CHUNKS, False, pl.ds(1, 3), pl.ds(0, HALF))
    far_units = (
        (CHUNKS + 1, True, pl.ds(0, QUARTERS - 1), pl.ds(0, CHUNKS - 1)),
        (CHUNKS + 2, True, pl.ds(0, QUARTERS - 1), pl.ds(CHUNKS - 1, 1)),
        (CHUNKS + 3, True, pl.ds(QUARTERS - 1, 1), pl.ds(0, HALF)),
        (CHUNKS + 4, True, pl.ds(QUARTERS - 1, 1), pl.ds(HALF, HALF)),
    )

    def own_part(unit, c, x, y):
        _, far, i, j = unit
        return (far_part, (c, x, y, i, j)) if far else (part, (c, i, j, x, y))

    def from_core(unit, x):
        _, far, i, j = unit
        return (far_core_in, (x, slice(None), i, j)) if far else (core_in, (i, j, x))

    def from_row(unit, k):
        _, far, i, j = unit
        return (far_row_in, (k, slice(None), i, j)) if far else (row_in, (k, i, j))

    def from_pair(unit):
        _, far, i, j = unit
        return (far_pair_in, (i, j)) if far else (pair_in, (i, j))

    def at(place):
        return place[0].at[place[1]]

    def read(place):
        return place[0][place[1]]

    every = slice(None)

    def core_copy(unit):
        sem = unit[0]
        return remote(
            at(own_part(unit, 1 - core, every, every)), at(from_core(unit, every)),
            core_send.at[sem], core_recv.at[sem], other_core(),
        )

    def row_copy(unit, step):
        sem = unit[0]
        return remote(
            at(own_part(unit, core, lax.rem(row + step, n_row), every)), at(from_row(unit, step - 1)),
            row_send.at[sem], row_recv.at[sem], in_row(step),
        )

    def row_copies(unit):
        sem = unit[0]
        block = at(from_row(unit, every))
        return remote(block, block, row_send.at[sem], row_recv.at[sem], in_row(1))

    def pair_copy(unit):
        sem = unit[0]
        return remote(
            at(own_part(unit, core, row, 1 - pair)), at(from_pair(unit)),
            pair_send.at[sem], pair_recv.at[sem], other_pair(),
        )

    def start_sum(unit):
        core_copy(unit).start()

    def sum_cores(unit):
        core_copy(unit).wait_recv()

        @pl.loop(0, n_row)
        def _(x):
            ref, index = own_part(unit, core, x, every)
            ref[index] = ref[index] + read(from_core(unit, x))

        for step in range(1, n_row):
            row_copy(unit, step).start()

    def sum_row(unit):
        row_copies(unit).wait_recv()
        ref, index = own_part(unit, core, row, every)
        value = ref[index]
        for k in range(n_row - 1):
            value = value + read(from_row(unit, k))
        ref[index] = value
        pair_copy(unit).start()

    def send_back(src, dst, sem, step):
        remote(src, dst, ret_send.at[sem], ret_recv.at[sem], along(step)).start()

    def sum_pair(unit):
        pair_copy(unit).wait_recv()
        _, far, i, j = unit
        value = read(own_part(unit, core, row, pair)) + read(from_pair(unit))
        if far:
            far_total[i, j] = value
            send_back(far_total.at[i, j], far_back.at[i, j], 2, 1)
            return
        total[i, j] = value
        low, high = i.start, i.start + i.size
        near_home = pl.ds(low, min(high, 2) - low)
        send_back(total.at[near_home, j], back_near.at[near_home, j], 0, 1)
        if high > 2:
            send_back(total.at[pl.ds(2, 2), j], back_far.at[:, j], 1, 2)

    def wait_sum(unit):
        core_copy(unit).wait_send()
        row_copies(unit).wait_send()
        pair_copy(unit).wait_send()

    def advance(ready, stage):
        @pl.when(jnp.logical_and(ready >= 0, ready < HALF))
        def _():
            stage(near_unit(ready))

        @pl.when(ready == HALF - 1)
        def _():
            stage(first_unit)

        @pl.when(jnp.logical_and(ready >= HALF, ready < CHUNKS - 1))
        def _():
            stage(whole_unit(ready))

        @pl.when(ready == CHUNKS - 2)
        def _():
            stage(far_units[0])

    barrier = pltpu.get_barrier_semaphore()
    for step in (-2, -1, 1, 2):
        pl.semaphore_signal(barrier, inc=1, device_id=along(step), device_id_type=MESH)

    for device in (other_core(), other_pair()) + tuple(in_row(step) for step in range(1, n_row)):
        pl.semaphore_signal(barrier, inc=1, device_id=device, device_id_type=MESH)
    pl.semaphore_wait(barrier, 4 + 2 + n_row - 1)

    for chunk in range(AHEAD):
        residents(chunk).start()
    load = pltpu.make_async_copy(grads, grads_v, load_sem)
    load.start()
    load.wait()

    count = grads_v.shape[0]
    some_rows = owners * own

    def take(step, block, chunk):
        line = lax.broadcasted_iota(jnp.int32, (some_rows, count), 0) + (offsets[step] + chunk * some_rows)
        source = lax.broadcasted_iota(jnp.int32, (some_rows, count), 1)
        pick = jnp.where(line == source, jnp.sqrt(resid[...]), 0.0)

        @pl.loop(0, depth // PICKED)
        def _(i):
            cols = pl.ds(pl.multiple_of(i * PICKED, PICKED), PICKED)
            value = lax.dot_general(
                pick,
                grads_v[:, cols],
                (((1,), (0,)), ((), ())),
                precision=lax.Precision.HIGH,
                preferred_element_type=jnp.float32,
            )
            block[pl.ds(chunk * owners, owners), :, cols] = value.reshape(owners, own, PICKED)

    @pl.loop(0, AHEAD)
    def _(chunk):
        take(1, mid, chunk)
        take(2, far, chunk)
        mid_visit(chunk).start()
        far_cut_visit(chunk).start()

    @pl.loop(0, QUARTERS)
    def _(chunk):
        take(0, near_v, chunk)

    def whole(ref):
        return ref[...].reshape(n_feat * own, ref.shape[2])

    def keep(value, tile, c):
        value = value.reshape(n_row, 2, 2, own, rows)
        for k in range(2):
            part[k, tile, c] = value[:, :, k]

    def near_tile(c):
        keep(product(whole(near_v), res_v[c]), 0, c)

    def mid_tile(c):
        keep(product(whole(mid_v), res_v[c, :, pl.ds(0, wide)]), 1, c)

    def cut_tiles(c):
        relay(c).wait_recv()
        block = res_far_v[c]
        keep(product(mid[:, :, pl.ds(wide, narrow)].reshape(n_feat * own, narrow), block), 2, c)
        keep(product(whole(far_far_v), block), 3, c)

    def far_tile(q, c):
        value = product(far_v[q].reshape(n_feat * quarter, wide), res_v[c, :, pl.ds(0, wide)])
        value = value.reshape(n_row, 2, 2, quarter, rows)
        for k in range(2):
            far_part[k, :, :, q, c] = value[:, :, k]

    @pl.loop(0, CHUNKS - 1)
    def _(t):
        residents(t).wait_recv()
        relay(t).start()
        residents(t).wait_send()

        @pl.when(t + AHEAD < CHUNKS)
        def _():
            residents(t + AHEAD).start()

        near_tile(t)

        @pl.when(t < QUARTERS)
        def _():
            mid_visit(t).wait_recv()
            far_cut_visit(t).wait_recv()

            @pl.when(t + AHEAD < QUARTERS)
            def _():
                take(1, mid, t + AHEAD)
                take(2, far, t + AHEAD)

            start_visit(t + AHEAD)

        @pl.loop(jnp.where(t < HALF - 1, t + 1, jnp.where(t == HALF - 1, 0, t)), t + 1)
        def _(c):
            mid_tile(c)

        @pl.when(t >= QUARTERS)
        def _():
            far_visit(t).wait_recv()
            start_visit(t + AHEAD)
            q = t - QUARTERS

            @pl.loop(0, t + q + 1)
            def _(i):
                earlier = i < t
                far_tile(jnp.where(earlier, q, i - t), jnp.where(earlier, i, t))

        @pl.loop(jnp.where(t < HALF - 1, t + 1, jnp.where(t == HALF - 1, 0, t)), t + 1)
        def _(c):
            cut_tiles(c)

        advance(t, start_sum)
        advance(t - 2, sum_row)
        advance(t - 1, sum_cores)

    end = CHUNKS - 1
    residents(end).wait_recv()
    relay(end).start()
    residents(end).wait_send()
    near_tile(end)
    mid_tile(end)
    advance(jnp.int32(end - 1), sum_cores)
    advance(jnp.int32(end - 2), sum_row)

    @pl.loop(0, end - 2)
    def _(ready):
        advance(ready, sum_pair)

    for q in range(QUARTERS - 1):
        far_tile(q, end)
    start_sum(far_units[1])
    cut_tiles(end)
    start_sum(whole_unit(end))
    advance(jnp.int32(end - 1), sum_row)
    for stage in (sum_cores, sum_row):
        stage(far_units[1])
        stage(whole_unit(end))

    @pl.loop(end - 2, end)
    def _(ready):
        advance(ready, sum_pair)

    for unit in (far_units[1], whole_unit(end)):
        sum_pair(unit)
    far_visit(end).wait_recv()

    for half in range(2):

        @pl.loop(half * HALF, (half + 1) * HALF)
        def _(c):
            far_tile(QUARTERS - 1, c)

        start_sum(far_units[2 + half])

    for stage in (sum_cores, sum_row, sum_pair):
        for unit in far_units[2:]:
            stage(unit)

    remote(total.at[pl.ds(0, 2)], back_near, ret_send.at[0], ret_recv.at[0], along(1)).wait()
    remote(total.at[pl.ds(2, 2)], back_far, ret_send.at[1], ret_recv.at[1], along(2)).wait()
    remote(far_total, far_back, ret_send.at[2], ret_recv.at[2], along(1)).wait()
    for c in range(CHUNKS):
        cols = pl.ds(c * rows, rows)
        weight = resid[:, cols]
        tiles = (
            back_near[0, c],
            back_near[1, c] + back_far[0, c],
            far_back[:, c].reshape(own, rows) + back_far[1, c],
        )
        for step, dots in enumerate(tiles):
            out[step, :, cols] = dots * dots * weight

    @pl.loop(0, CHUNKS)
    def _(t):
        relay(t).wait_send()

        @pl.when(t < HALF)
        def _():
            wait_sum(near_unit(t))

        @pl.when(t >= HALF)
        def _():
            wait_sum(whole_unit(t))

    for unit in (first_unit,) + far_units:
        wait_sum(unit)

    @pl.loop(0, QUARTERS)
    def _(t):
        mid_visit(t).wait_send()
        far_cut_visit(t).wait_send()
        far_visit(t + QUARTERS).wait_send()


def shards(grads, resid, offsets):
    n_feat = lax.axis_size("feat")
    count, depth = grads.shape
    own = GROUP // n_feat
    rows = count // CHUNKS
    narrow = depth // 4
    wide = depth - narrow
    f32 = jnp.float32
    units = CHUNKS + 5
    dma = pltpu.SemaphoreType.DMA
    xs = n_feat // 4
    far = (QUARTERS, CHUNKS, own // QUARTERS, rows)
    return pl.pallas_call(
        kernel,
        out_shape=jax.ShapeDtypeStruct((STEPS, own, count), f32),
        in_specs=[
            pl.BlockSpec(memory_space=pltpu.SMEM),
            pl.BlockSpec(memory_space=pl.ANY),
            pl.BlockSpec(memory_space=pltpu.VMEM),
        ],
        out_specs=pl.BlockSpec(memory_space=pltpu.VMEM),
        scratch_shapes=[
            pltpu.VMEM((count, depth), f32),
            pltpu.VMEM((n_feat, own, depth), f32),
            pltpu.VMEM((n_feat, own, depth), f32),
            pltpu.VMEM((n_feat, own, depth), f32),
            pltpu.VMEM((n_feat, own, wide), f32),
            pltpu.VMEM((QUARTERS, n_feat, own // QUARTERS, wide), f32),
            pltpu.VMEM((n_feat, own, narrow), f32),
            pltpu.VMEM((CHUNKS, rows, depth), f32),
            pltpu.VMEM((CHUNKS, rows, narrow), f32),
            pltpu.VMEM((2, 4, CHUNKS, xs, 2, own, rows), f32),
            pltpu.VMEM((4, CHUNKS, xs, 2, own, rows), f32),
            pltpu.VMEM((xs - 1, 4, CHUNKS, 2, own, rows), f32),
            pltpu.VMEM((4, CHUNKS, own, rows), f32),
            pltpu.VMEM((4, CHUNKS, own, rows), f32),
            pltpu.VMEM((2, CHUNKS, own, rows), f32),
            pltpu.VMEM((2, CHUNKS, own, rows), f32),
            pltpu.VMEM((2, xs, 2) + far, f32),
            pltpu.VMEM((xs, 2) + far, f32),
            pltpu.VMEM((xs - 1, 2) + far, f32),
            pltpu.VMEM(far, f32),
            pltpu.VMEM(far, f32),
            pltpu.VMEM(far, f32),
            dma((CHUNKS,)), dma((CHUNKS,)), dma((CHUNKS,)), dma((CHUNKS,)),
            dma((CHUNKS,)), dma((CHUNKS,)), dma((QUARTERS,)), dma((QUARTERS,)),
            dma((units,)), dma((units,)), dma((units,)), dma((units,)), dma((units,)), dma((units,)), dma((3,)), dma((3,)), dma,
        ],
        compiler_params=pltpu.CompilerParams(
            collective_id=0, has_side_effects=True, vmem_limit_bytes=62 * 2**20
        ),
    )(offsets, grads, resid[None, :])


def solution(mesh):
    return jax.shard_map(
        shards,
        mesh=mesh,
        in_specs=(P("ex", "feat"), P("ex"), P()),
        out_specs=P(None, "feat", "ex"),
        check_vma=False,
    )
```
